32 devices in a mesh: dp: 4 (over y, core), row: 2 (over x), col: 4 (over z).
Axes of the slice: x: 2, y: 2, z: 4, core: 2. Of those that a mesh axis runs over, the one named last changes fastest.
Arguments:
- source_rows: bfloat16 [1536, 12288], P(('dp', 'col'), 'row'), may hold values from -6 to 6
- segments: int32 [16, 96], P(('dp', 'col')), may hold values from 0 to 95, as said below
- send_slots: int32 [16, 4, 23], P(('dp', 'col')), may hold values from 0 to 95, as said below
- send_counts: int32 [4, 4, 4], P('col'), may hold values from 1 to 23, as said below
- block_weight: bfloat16 [16, 768, 3072], P('row', None, 'col'), may hold values from -0.21875 to 0.21875
- lowrank_in: bfloat16 [16, 768, 512], P('row'), may hold values from -0.0546875 to 0.0546875
- lowrank_out: bfloat16 [512, 16, 3072], P(None, 'row', 'col'), may hold values from -0.25 to 0.25
- cotangent: bfloat16 [768, 16, 3072], P('dp', 'row', 'col'), may hold values from -6 to 6
Outputs:
- activation: bfloat16 [768, 16, 3072], P('dp', 'row', 'col')
- input_grad: bfloat16 [768, 12288], P(('dp', 'col'), 'row')
- block_grad: float32 [768, 16, 3072], P('dp', 'row', 'col')
- lowrank_out_grad: float32 [512, 16, 3072], P('dp', 'row', 'col')
The draws below stay inside these ranges and needn't reach their ends.
Inputs may be any that keep to these rules, and one draw needn't show every extreme that they name: For every col index c and destination e, the entries send_counts[c, :, e] sum to 48. For source device s = d * 4 + c, the first send_counts[c, d, e] entries of send_slots[s, e] are distinct slots, and over all e they name each of the slots 0 to L_s - 1 exactly once (L_s as in the reference program); the entries past the count are slot numbers that carry nothing. `segments`: along one device's slots the ids never fall.
All inputs are finite; a program needn't handle non-finite values.
Results may differ from the reference program's by a relative error of at most 0.024.
Values may be sent and summed in bfloat16 or wider, within the bound.
A program may use at most 128 MiB of HBM per device.

```python
import jax
import jax.numpy as jnp
from jax import lax

D = 12288
NB = 16
RANK = 512
TOK_DEV = 48
DB = 768
HB = 3072
SLOTS = 96
CAP = 23
TOKENS = 768
SOURCE_ROWS = 1536
N_DP = 4
N_ROW = 2
N_COL = 4


def plan_counts(key):
    even_share = TOK_DEV // N_DP
    max_swing = even_share - 1
    key_load, key_pick, key_order, key_pair = jax.random.split(jax.random.fold_in(key, 11), 4)
    swing_size = max_swing - jax.random.randint(key_load, (N_COL, N_DP), 0, even_share // 2 + 1)
    picked = jax.random.randint(key_pick, (N_COL, 1), 0, N_DP)
    swing_size = jnp.where(jnp.arange(N_DP)[None, :] == picked, max_swing, swing_size)
    orders = jax.vmap(lambda sub_key: jax.random.permutation(sub_key, N_DP))(jax.random.split(key_order, N_COL))
    pair_on = jax.random.randint(key_pair, (N_COL, N_DP // 2), 0, 2)
    pair_on = jnp.where(jnp.arange(N_DP // 2)[None, :] == 0, 1, pair_on)
    signed = jnp.repeat(pair_on, 2, axis=1) * jnp.tile(jnp.array([1, -1], jnp.int32), N_DP // 2)[None, :]
    inverse = jnp.argsort(orders, axis=1)
    shifts = jnp.take_along_axis(signed, inverse, axis=1)
    return (even_share + shifts[:, :, None] * swing_size[:, None, :]).astype(jnp.int32)


def draw_send_counts(key, part):
    return plan_counts(key)


def draw_send_slots(key, part):
    counts = plan_counts(key)
    per_source = jnp.transpose(counts, (1, 0, 2)).reshape(N_DP * N_COL, N_DP)
    alive_count = jnp.sum(per_source, axis=1)
    source_keys = jax.random.split(jax.random.fold_in(key, 23), N_DP * N_COL)

    def one_source(sub_key, alive_total, row_counts):
        shuffled = jax.random.permutation(sub_key, SLOTS)
        ranked = shuffled[jnp.argsort((shuffled >= alive_total).astype(jnp.int32), stable=True)]
        starts = jnp.cumsum(row_counts) - row_counts
        places = jnp.minimum(starts[:, None] + jnp.arange(CAP)[None, :], SLOTS - 1)
        return ranked[places]
    return jax.vmap(one_source)(source_keys, alive_count, per_source).astype(jnp.int32)


def draw_segments(key, part):
    doc_keys = jax.random.split(jax.random.fold_in(key, 37), N_DP * N_COL)

    def one_device(sub_key):
        lengths = jax.random.randint(sub_key, (SLOTS // 4 + 1,), 4, 65)
        doc_ends = jnp.cumsum(lengths)
        doc_index = jnp.sum((doc_ends[None, :] <= jnp.arange(SLOTS)[:, None]).astype(jnp.int32), axis=1)
        return jnp.minimum(jnp.take(doc_ends, doc_index) - 1, SLOTS - 1)
    return jax.vmap(one_device)(doc_keys).astype(jnp.int32)


def block_levels(stream_key, dims, shards, least, top_value):
    def one(axis_at, parts):
        draws = jax.random.uniform(jax.random.fold_in(jax.random.fold_in(stream_key, 6), axis_at), (parts,), jnp.float32, least / len(shards), top_value / len(shards))
        return jnp.repeat(jnp.exp(draws), dims[axis_at] // parts).reshape((-1,) + (1,) * (len(dims) - axis_at - 1))

    factor_of = one(*shards[0])
    for cut in shards[1:]:
        factor_of = factor_of * one(*cut)
    return factor_of


def scatter_about(rng, dims, deviation, most, pieces=(), kind=jnp.bfloat16):
    entries = jax.random.normal(rng, dims, jnp.float32) * deviation
    if len(pieces) > 0:
        entries = block_levels(rng, dims, pieces, -0.22, 0.18) * entries
    return jnp.clip(entries, min=-most, max=most).astype(kind)


def setup_inputs(seed: int = 0) -> dict:
    streams_of = jax.random.split(jax.random.key(seed), 9)
    source_rows = scatter_about(streams_of[0], (SOURCE_ROWS, D), 1.0, 6.0, ((0, 16), (1, 2)))
    segments = draw_segments(jax.random.fold_in(streams_of[8], 71), 0)
    send_slots = draw_send_slots(jax.random.fold_in(streams_of[8], 71), 0)
    send_counts = draw_send_counts(jax.random.fold_in(streams_of[8], 71), 0)
    block_weight = scatter_about(streams_of[4], (NB, DB, HB), DB ** -0.5, 0.21875, ((0, 2), (2, 4)))
    lowrank_in = scatter_about(streams_of[5], (NB, DB, RANK), D ** -0.5, 0.0546875, ((0, 2),))
    lowrank_out = scatter_about(streams_of[6], (RANK, NB, HB), RANK ** -0.5, 0.25, ((1, 2), (2, 4)))
    cotangent = scatter_about(streams_of[7], (TOKENS, NB, HB), 1.0, 6.0, ((0, 4), (1, 2), (2, 4)))
    return {"source_rows": source_rows, "segments": segments, "send_slots": send_slots, "send_counts": send_counts, "block_weight": block_weight, "lowrank_in": lowrank_in, "lowrank_out": lowrank_out, "cotangent": cotangent}


def gelu_pair(pre_act):
    cubic = pre_act * pre_act * pre_act
    tanh_val = jnp.tanh(0.7978845608 * (pre_act + 0.044715 * cubic))
    activation = 0.5 * pre_act * (1.0 + tanh_val)
    derivative = 0.5 * (1.0 + tanh_val) + 0.5 * pre_act * (1.0 - tanh_val * tanh_val) * 0.7978845608 * (1.0 + 0.134145 * pre_act * pre_act)
    return activation, derivative


def round_trip(values):
    return lax.optimization_barrier(values.astype(jnp.bfloat16)).astype(jnp.float32)


def doc_weights(segments, alive_count):
    slot_ids = jnp.arange(SLOTS, dtype=jnp.int32)
    is_alive = slot_ids[None, :] < alive_count[:, None]
    same_doc = (segments[:, :, None] == segments[:, None, :]) & is_alive[:, None, :]
    doc_length = jnp.sum(same_doc.astype(jnp.float32), axis=2)
    return (32.0 / (16.0 + doc_length)).astype(jnp.bfloat16)


def reference(source_rows, segments, send_slots, send_counts, block_weight, lowrank_in, lowrank_out, cotangent):
    per_source = jnp.transpose(send_counts, (1, 0, 2))
    alive_count = jnp.sum(per_source, axis=2).reshape(N_DP * N_COL).astype(jnp.int32)
    weights = doc_weights(segments, alive_count)
    starts = (jnp.cumsum(send_counts, axis=1) - send_counts).astype(jnp.int32)
    positions = jnp.arange(TOK_DEV, dtype=jnp.int32)
    passed = (starts[:, :, :, None] <= positions[None, None, None, :]).astype(jnp.int32)
    sender = (jnp.sum(passed, axis=1) - 1).astype(jnp.int32)
    start_table = jnp.transpose(starts, (0, 2, 1))
    offset = (positions[None, None, :] - jnp.take_along_axis(start_table, sender, axis=2)).astype(jnp.int32)
    col_ids = jnp.arange(N_COL, dtype=jnp.int32)[:, None, None]
    dest_ids = jnp.arange(N_DP, dtype=jnp.int32)[None, :, None]
    source_dev = (sender * N_COL + col_ids).astype(jnp.int32)
    chosen_slot = send_slots[source_dev, dest_ids, offset].astype(jnp.int32)
    flat_source = (source_dev * SLOTS + chosen_slot).astype(jnp.int32)
    source_index = jnp.transpose(flat_source, (1, 0, 2)).reshape(TOKENS)
    moved_rows = source_rows[source_index]
    token_weight = weights.reshape(N_DP * N_COL * SLOTS)[source_index]

    flat_in = lowrank_in.reshape(D, RANK)
    low_code = jnp.dot(moved_rows, flat_in, preferred_element_type=jnp.float32).astype(jnp.bfloat16)
    per_row = NB // N_ROW
    slice_width = HB // N_COL
    rows_by_group = moved_rows.reshape(TOKENS, N_ROW, per_row, DB).transpose(1, 0, 2, 3)
    blocks_by_group = block_weight.reshape(N_ROW, per_row, DB, HB)
    out_by_group = lowrank_out.reshape(RANK, N_ROW, per_row, HB).transpose(1, 0, 2, 3)
    cot_by_group = cotangent.reshape(TOKENS, N_ROW, per_row, HB).transpose(1, 0, 2, 3)
    wide_weight = token_weight.astype(jnp.float32)[:, None, None]
    low_wide = low_code.astype(jnp.float32)

    def one_group(items):
        group_rows, group_blocks, group_out, group_cot = items
        rows_wide = group_rows.astype(jnp.float32)
        blocks_wide = group_blocks.astype(jnp.float32)
        out_wide = group_out.astype(jnp.float32)
        pre_act = jnp.einsum("tbi,bij->tbj", rows_wide, blocks_wide) + jnp.einsum("tk,kbj->tbj", low_wide, out_wide)
        activation, derivative = gelu_pair(pre_act)
        grad_pre = (wide_weight * group_cot.astype(jnp.float32) * derivative).astype(jnp.bfloat16)
        grad_wide = grad_pre.astype(jnp.float32)
        grad_split = grad_wide.reshape(TOKENS, per_row, N_COL, slice_width)
        input_parts = jnp.einsum("tbcj,bicj->tcbi", grad_split, blocks_wide.reshape(per_row, DB, N_COL, slice_width))
        input_term = jnp.sum(round_trip(input_parts), axis=1)
        low_parts = jnp.einsum("tbcj,kbcj->tck", grad_split, out_wide.reshape(RANK, per_row, N_COL, slice_width))
        low_term = jnp.sum(round_trip(low_parts), axis=1)
        grad_groups = grad_wide.reshape(N_DP, TOKENS // N_DP, per_row, HB)
        block_parts = jnp.einsum("gtbi,gtbj->gibj", rows_wide.reshape(N_DP, TOKENS // N_DP, per_row, DB), grad_groups)
        block_sum = jnp.sum(round_trip(block_parts), axis=0)
        out_parts = jnp.einsum("gtk,gtbj->gkbj", low_wide.reshape(N_DP, TOKENS // N_DP, RANK), grad_groups)
        out_sum = jnp.sum(round_trip(out_parts), axis=0)
        return activation.astype(jnp.bfloat16), input_term, low_term, block_sum, out_sum

    acts, input_terms, low_terms, block_sums, out_sums = lax.map(one_group, (rows_by_group, blocks_by_group, out_by_group, cot_by_group))
    activation = acts.transpose(1, 0, 2, 3).reshape(TOKENS, NB, HB)
    input_term = input_terms.transpose(1, 0, 2, 3).reshape(TOKENS, D)
    low_grad = jnp.sum(low_terms, axis=0).astype(jnp.bfloat16)
    low_back = lax.dot_general(low_grad, flat_in, (((1,), (1,)), ((), ())), preferred_element_type=jnp.float32)
    input_grad = (input_term + low_back).astype(jnp.bfloat16)
    block_grad = block_sums.transpose(1, 0, 2, 3).reshape(DB, NB, HB)
    lowrank_out_grad = out_sums.transpose(1, 0, 2, 3).reshape(RANK, NB, HB)
    return activation, input_grad, block_grad, lowrank_out_grad
```

```python
import functools

import jax
import jax.numpy as jnp
from jax import lax
from jax.experimental import pallas as pl
from jax.experimental.pallas import tpu as pltpu
from jax.sharding import PartitionSpec as P

F32 = jnp.float32
BF16 = jnp.bfloat16


def dot(left, right, left_dim, right_dim):
    return lax.dot_general(
        left, right, (((left_dim,), (right_dim,)), ((), ())), preferred_element_type=F32
    )


def block_kernel(rows, weight, low, low_out, cot, tok_weight, act, grad, in_term, low_term):
    pre = dot(rows[...], weight[0], 1, 0) + dot(low[...], low_out[0], 1, 0)
    square = pre * pre
    tanh_val = jnp.tanh(0.7978845608 * (pre + 0.044715 * (square * pre)))
    half = 0.5 * (1.0 + tanh_val)
    act[0] = (pre * half).astype(BF16)
    slope = half + 0.5 * pre * (1.0 - tanh_val * tanh_val) * 0.7978845608 * (
        1.0 + 0.134145 * square
    )
    grad_pre = (tok_weight[...] * cot[0].astype(F32) * slope).astype(BF16)
    grad[0] = grad_pre
    in_term[...] = dot(grad_pre, weight[0], 1, 1).astype(BF16)
    part = dot(grad_pre, low_out[0], 1, 1)

    @pl.when(pl.program_id(0) == 0)
    def _():
        low_term[...] = part

    @pl.when(pl.program_id(0) > 0)
    def _():
        low_term[...] += part


def block_chunk(rows, row_base, weight, low, low_out, cot, tok_weight, base, count):
    tokens = rows.shape[0]
    n_blocks, width_in, width_out = weight.shape
    rank = low.shape[1]
    return pl.pallas_call(
        block_kernel,
        grid=(count,),
        in_specs=[
            pl.BlockSpec((tokens, width_in), lambda b: (0, row_base + b)),
            pl.BlockSpec((1, width_in, width_out), lambda b: (base + b, 0, 0)),
            pl.BlockSpec((tokens, rank), lambda b: (0, 0)),
            pl.BlockSpec((1, rank, width_out), lambda b: (base + b, 0, 0)),
            pl.BlockSpec((1, tokens, width_out), lambda b: (base + b, 0, 0)),
            pl.BlockSpec((tokens, 1), lambda b: (0, 0)),
        ],
        out_specs=[
            pl.BlockSpec((1, tokens, width_out), lambda b: (b, 0, 0)),
            pl.BlockSpec((1, tokens, width_out), lambda b: (b, 0, 0)),
            pl.BlockSpec((tokens, width_in), lambda b: (0, b)),
            pl.BlockSpec((tokens, rank), lambda b: (0, 0)),
        ],
        out_shape=[
            jax.ShapeDtypeStruct((count, tokens, width_out), BF16),
            jax.ShapeDtypeStruct((count, tokens, width_out), BF16),
            jax.ShapeDtypeStruct((tokens, count * width_in), BF16),
            jax.ShapeDtypeStruct((tokens, rank), F32),
        ],
        cost_estimate=pl.CostEstimate(
            flops=4 * count * tokens * width_out * (width_in + rank),
            bytes_accessed=2 * count * width_out * (width_in + rank + 3 * tokens),
            transcendentals=count * tokens * width_out,
        ),
    )(rows, weight, low, low_out, cot, tok_weight)


def split_kernel(n_parts, rows, out):
    part = out.shape[3]
    value = rows[...]
    for e in range(n_parts):
        out[e, 0] = value[:, e * part : (e + 1) * part]


def split_rows(rows, n_blocks, n_parts):
    tokens, width = rows.shape
    block_in = width // n_blocks
    part = block_in // n_parts
    return pl.pallas_call(
        functools.partial(split_kernel, n_parts),
        grid=(n_blocks,),
        in_specs=[pl.BlockSpec((tokens, block_in), lambda b: (0, b))],
        out_specs=pl.BlockSpec((n_parts, 1, tokens, part), lambda b: (0, b, 0, 0)),
        out_shape=jax.ShapeDtypeStruct((n_parts, n_blocks, tokens, part), BF16),
        cost_estimate=pl.CostEstimate(
            flops=0, bytes_accessed=4 * tokens * width, transcendentals=0
        ),
    )(rows)


def weight_kernel(n_groups, halves, chunks, *refs):
    rows = refs[: n_groups * halves]
    refs = refs[n_groups * halves :]
    lows = refs[:n_groups]
    grads = refs[n_groups : n_groups + n_groups * chunks]
    block_out, low_out = refs[n_groups + n_groups * chunks :]
    n_blocks = block_out.shape[1]
    per_chunk = n_blocks // chunks
    per_half = n_blocks // halves
    for b in range(n_blocks):
        block_sum = None
        low_sum = None
        for g in range(n_groups):
            grad = grads[g * chunks + b // per_chunk][b % per_chunk]
            row = rows[g * halves + b // per_half][b % per_half]
            block_part = dot(row, grad, 0, 0)
            low_part = dot(lows[g][...], grad, 0, 0)
            block_sum = block_part if g == 0 else block_sum + block_part
            low_sum = low_part if g == 0 else low_sum + low_part
        block_out[:, b, :] = block_sum
        low_out[:, b, :] = low_sum


def weight_grads(rows, lows, grads):
    n_groups = len(rows)
    halves = len(rows[0])
    chunks = len(grads[0])
    per_half, tokens, part = rows[0][0].shape
    per_chunk, _, width = grads[0][0].shape
    n_blocks = per_chunk * chunks
    rank = lows[0].shape[1]
    tile = 256 if width % 256 == 0 else width
    flat_rows = [x for group in rows for x in group]
    flat_grads = [x for group in grads for x in group]
    return pl.pallas_call(
        functools.partial(weight_kernel, n_groups, halves, chunks),
        grid=(width // tile,),
        in_specs=[pl.BlockSpec((per_half, tokens, part), lambda j: (0, 0, 0))] * len(flat_rows)
        + [pl.BlockSpec((tokens, rank), lambda j: (0, 0))] * n_groups
        + [pl.BlockSpec((per_chunk, tokens, tile), lambda j: (0, 0, j))] * len(flat_grads),
        out_specs=[
            pl.BlockSpec((part, n_blocks, tile), lambda j: (0, 0, j)),
            pl.BlockSpec((rank, n_blocks, tile), lambda j: (0, 0, j)),
        ],
        out_shape=[
            jax.ShapeDtypeStruct((part, n_blocks, width), F32),
            jax.ShapeDtypeStruct((rank, n_blocks, width), F32),
        ],
        cost_estimate=pl.CostEstimate(
            flops=2 * n_groups * tokens * n_blocks * width * (part + rank),
            bytes_accessed=2 * n_groups * tokens * n_blocks * width
            + 4 * (part + rank) * n_blocks * width,
            transcendentals=0,
        ),
    )(*flat_rows, *lows, *flat_grads)


def doc_weights(segment_row, alive_count):
    slot_ids = jnp.arange(segment_row.shape[0], dtype=jnp.int32)
    is_alive = slot_ids < alive_count
    same_doc = (segment_row[:, None] == segment_row[None, :]) & is_alive[None, :]
    doc_length = jnp.sum(same_doc.astype(F32), axis=1)
    return (32.0 / (16.0 + doc_length)).astype(BF16)


def swap(value, axis, mask):
    return lax.ppermute(value, axis, [(s, s ^ mask) for s in range(lax.axis_size(axis))])


def row_total(partial_sum):
    mine = partial_sum.astype(BF16)
    if lax.axis_size("row") == 2:
        return mine.astype(F32) + swap(mine, "row", 1).astype(F32)
    return lax.psum(mine, "row").astype(F32)


def gather_groups(value, masks):
    held = [value]
    for mask in masks:
        held = held + [swap(x, "dp", mask) for x in held]
    return held


def local(
    source_rows, segments, send_slots, send_counts, block_weight, lowrank_in, lowrank_out, cotangent
):
    n_data = lax.axis_size("dp")
    n_col = lax.axis_size("col")
    my_data = lax.axis_index("dp")
    n_blocks, block_in, block_out = block_weight.shape
    rank_width = lowrank_in.shape[2]
    group_rows = cotangent.shape[0]
    own_rows = group_rows // n_col
    count_table = send_counts[0]
    slot_table = send_slots[0]
    outgoing = jnp.take(source_rows, slot_table, axis=0)
    incoming = lax.all_to_all(outgoing, "dp", split_axis=0, concat_axis=0, tiled=True)
    capacity = slot_table.shape[1]
    arrivals = lax.dynamic_index_in_dim(count_table, my_data, 1, keepdims=False)
    starts = jnp.cumsum(arrivals) - arrivals
    positions = jnp.arange(own_rows, dtype=jnp.int32)
    sender = jnp.sum((starts[None, :] <= positions[:, None]).astype(jnp.int32), axis=1) - 1
    offset = positions - jnp.take(starts, sender)
    flat_index = sender * capacity + offset
    my_rows = jnp.take(incoming.reshape(n_data * capacity, incoming.shape[2]), flat_index, axis=0)

    segment_row, _ = lax.optimization_barrier((segments[0], outgoing))
    my_alive = jnp.sum(lax.dynamic_index_in_dim(count_table, my_data, 0, keepdims=False))
    weights = doc_weights(segment_row, my_alive)
    out_weights = jnp.take(weights, slot_table, axis=0)
    in_weights = lax.all_to_all(out_weights, "dp", split_axis=0, concat_axis=0, tiled=True)
    my_weights = jnp.take(in_weights.reshape(n_data * capacity), flat_index, axis=0)

    flat_in = lowrank_in.reshape(n_blocks * block_in, rank_width)
    own_part = jnp.dot(my_rows, flat_in, preferred_element_type=F32)
    own_low = row_total(own_part).astype(BF16)
    own_extra = jnp.concatenate(
        [own_low, jnp.broadcast_to(my_weights[:, None], (own_rows, 128))], axis=1
    )
    halves = 2
    half_width = n_blocks * block_in // halves
    panel_low = None
    panels = []
    for h in range(halves):
        piece = my_rows[:, h * half_width : (h + 1) * half_width]
        panels.append(lax.all_gather(piece, "col", axis=0, tiled=True))
        if h == 0:
            extra = lax.all_gather(own_extra, "col", axis=0, tiled=True)
            panel_low = extra[:, :rank_width]
            tok_weight = extra[:, rank_width : rank_width + 1].astype(F32)

    low_out_blocks = jnp.transpose(lowrank_out, (1, 0, 2))
    cot_blocks = jnp.transpose(cotangent, (1, 0, 2))

    masks = []
    bit = n_data // 2
    while bit:
        masks.append(bit)
        bit //= 2
    offsets = [0]
    for mask in masks:
        offsets = offsets + [k ^ mask for k in offsets]

    low_split = jnp.transpose(panel_low.reshape(group_rows, n_data, -1), (1, 0, 2))
    per_half = n_blocks // halves
    chunks = min(4, n_blocks)
    per_chunk = n_blocks // chunks
    acts, grads, in_terms, low_terms, row_parts = [], [], [], [], []
    for h in range(halves):
        row_parts.append(split_rows(panels[h], per_half, n_data))
    for c in range(chunks):
        h = c * per_chunk // per_half
        act, grad, in_term, low_term = block_chunk(
            panels[h],
            c * per_chunk - h * per_half,
            block_weight,
            panel_low,
            low_out_blocks,
            cot_blocks,
            tok_weight,
            c * per_chunk,
            per_chunk,
        )
        acts.append(act)
        grads.append(gather_groups(grad, masks))
        in_terms.append(in_term)
        low_terms.append(low_term)

    group_slices, group_lows = [], []
    for k in offsets:
        pieces = []
        for h in range(halves):
            piece = lax.dynamic_index_in_dim(row_parts[h], my_data ^ k, 0, keepdims=False)
            pieces.append(swap(piece, "dp", k) if k else piece)
        group_slices.append(pieces)
        low_piece = lax.dynamic_index_in_dim(low_split, my_data ^ k, 0, keepdims=False)
        group_lows.append(swap(low_piece, "dp", k) if k else low_piece)

    own_low_term = lax.psum_scatter(
        sum(low_terms).astype(BF16), "col", scatter_dimension=0, tiled=True
    )
    low_grad = row_total(own_low_term).astype(BF16)
    half_chunks = chunks // halves
    terms = []
    for h in range(halves):
        part = jnp.concatenate(in_terms[h * half_chunks : (h + 1) * half_chunks], axis=1)
        terms.append(lax.psum_scatter(part, "col", scatter_dimension=0, tiled=True))
    own_term = jnp.concatenate(terms, axis=1).astype(F32)
    input_grad = (own_term + dot(low_grad, flat_in, 1, 1)).astype(BF16)

    act_out = jnp.transpose(jnp.concatenate(acts, axis=0), (1, 0, 2))
    by_group = [[grads[c][g] for c in range(chunks)] for g in range(n_data)]
    block_grad, out_grad = weight_grads(group_slices, group_lows, by_group)
    return (act_out, input_grad, block_grad, out_grad)


def solution(mesh):
    in_specs = (
        P(("dp", "col"), "row"),
        P(("dp", "col"), None),
        P(("dp", "col"), None, None),
        P("col", None, None),
        P("row", None, "col"),
        P("row", None, None),
        P(None, "row", "col"),
        P("dp", "row", "col"),
    )
    out_specs = (
        P("dp", "row", "col"),
        P(("dp", "col"), "row"),
        P("dp", "row", "col"),
        P("dp", "row", "col"),
    )
    return jax.shard_map(local, mesh=mesh, in_specs=in_specs, out_specs=out_specs, check_vma=False)
```

```python
import functools

import jax
import jax.numpy as jnp
from jax import lax
from jax.experimental import pallas as pl
from jax.experimental.pallas import tpu as pltpu
from jax.sharding import PartitionSpec as P


F32 = jnp.float32
BF16 = jnp.bfloat16


def dot(left, right, left_dim, right_dim):
    return lax.dot_general(
        left, right, (((left_dim,), (right_dim,)), ((), ())), preferred_element_type=F32
    )


def block_kernel(rows, weight, low, low_out, cot, tok_weight, act, grad, in_term, low_term):
    pre = dot(rows[...], weight[0], 1, 0) + dot(low[...], low_out[0], 1, 0)
    square = pre * pre
    tanh_val = jnp.tanh(0.7978845608 * (pre + 0.044715 * (square * pre)))
    half = 0.5 * (1.0 + tanh_val)
    act[0] = (pre * half).astype(BF16)
    slope = half + 0.5 * pre * (1.0 - tanh_val * tanh_val) * 0.7978845608 * (
        1.0 + 0.134145 * square
    )
    grad_pre = (tok_weight[...] * cot[0].astype(F32) * slope).astype(BF16)
    grad[0] = grad_pre
    in_term[...] = dot(grad_pre, weight[0], 1, 1).astype(BF16)
    part = dot(grad_pre, low_out[0], 1, 1)

    @pl.when(pl.program_id(0) == 0)
    def _():
        low_term[...] = part

    @pl.when(pl.program_id(0) > 0)
    def _():
        low_term[...] += part


def block_chunk(rows, row_base, weight, low, low_out, cot, tok_weight, base, count):
    tokens = rows.shape[0]
    _, width_in, width_out = weight.shape
    rank = low.shape[1]
    return pl.pallas_call(
        block_kernel,
        grid=(count,),
        in_specs=[
            pl.BlockSpec((tokens, width_in), lambda b: (0, row_base + b)),
            pl.BlockSpec((1, width_in, width_out), lambda b: (base + b, 0, 0)),
            pl.BlockSpec((tokens, rank), lambda b: (0, 0)),
            pl.BlockSpec((1, rank, width_out), lambda b: (base + b, 0, 0)),
            pl.BlockSpec((1, tokens, width_out), lambda b: (base + b, 0, 0)),
            pl.BlockSpec((tokens, 1), lambda b: (0, 0)),
        ],
        out_specs=[
            pl.BlockSpec((1, tokens, width_out), lambda b: (b, 0, 0)),
            pl.BlockSpec((1, tokens, width_out), lambda b: (b, 0, 0)),
            pl.BlockSpec((tokens, width_in), lambda b: (0, b)),
            pl.BlockSpec((tokens, rank), lambda b: (0, 0)),
        ],
        out_shape=[
            jax.ShapeDtypeStruct((count, tokens, width_out), BF16),
            jax.ShapeDtypeStruct((count, tokens, width_out), BF16),
            jax.ShapeDtypeStruct((tokens, count * width_in), BF16),
            jax.ShapeDtypeStruct((tokens, rank), F32),
        ],
        cost_estimate=pl.CostEstimate(
            flops=4 * count * tokens * width_out * (width_in + rank),
            bytes_accessed=2 * count * width_out * (width_in + rank + 3 * tokens),
            transcendentals=count * tokens * width_out,
        ),
    )(rows, weight, low, low_out, cot, tok_weight)


def split_kernel(n_parts, offsets, me, rows, *outs):
    part = outs[0].shape[2]
    for out, k in zip(outs, offsets):
        for e in range(n_parts):

            @pl.when((me[0] ^ k) == e)
            def _(out=out, e=e):
                out[0] = rows[:, e * part : (e + 1) * part]


def split_rows(me, rows, n_blocks, offsets):
    tokens, width = rows.shape
    n_parts = len(offsets)
    block_in = width // n_blocks
    part = block_in // n_parts
    return pl.pallas_call(
        functools.partial(split_kernel, n_parts, offsets),
        grid_spec=pltpu.PrefetchScalarGridSpec(
            num_scalar_prefetch=1,
            grid=(n_blocks,),
            in_specs=[pl.BlockSpec((tokens, block_in), lambda b, me: (0, b))],
            out_specs=[pl.BlockSpec((1, tokens, part), lambda b, me: (b, 0, 0))] * n_parts,
        ),
        out_shape=[jax.ShapeDtypeStruct((n_blocks, tokens, part), BF16)] * n_parts,
        cost_estimate=pl.CostEstimate(
            flops=0, bytes_accessed=4 * tokens * width, transcendentals=0
        ),
    )(me, rows)


def weight_kernel(n_groups, halves, chunks, *refs):
    rows = refs[: n_groups * halves]
    refs = refs[n_groups * halves :]
    lows = refs[:n_groups]
    grads = refs[n_groups : n_groups + n_groups * chunks]
    block_out, low_out = refs[n_groups + n_groups * chunks :]
    n_blocks = block_out.shape[1]
    per_chunk = n_blocks // chunks
    per_half = n_blocks // halves
    for b in range(n_blocks):
        block_sum = None
        low_sum = None
        for g in range(n_groups):
            grad = grads[g * chunks + b // per_chunk][b % per_chunk]
            row = rows[g * halves + b // per_half][b % per_half]
            block_part = dot(row, grad, 0, 0)
            low_part = dot(lows[g][...], grad, 0, 0)
            block_sum = block_part if g == 0 else block_sum + block_part
            low_sum = low_part if g == 0 else low_sum + low_part
        block_out[:, b, :] = block_sum
        low_out[:, b, :] = low_sum


def weight_grads(rows, lows, grads):
    n_groups = len(rows)
    halves = len(rows[0])
    chunks = len(grads[0])
    per_half, tokens, part = rows[0][0].shape
    per_chunk, _, width = grads[0][0].shape
    n_blocks = per_chunk * chunks
    rank = lows[0].shape[1]
    tile = 256 if width % 256 == 0 else width
    flat_rows = [x for group in rows for x in group]
    flat_grads = [x for group in grads for x in group]
    return pl.pallas_call(
        functools.partial(weight_kernel, n_groups, halves, chunks),
        grid=(width // tile,),
        in_specs=[pl.BlockSpec((per_half, tokens, part), lambda j: (0, 0, 0))] * len(flat_rows)
        + [pl.BlockSpec((tokens, rank), lambda j: (0, 0))] * n_groups
        + [pl.BlockSpec((per_chunk, tokens, tile), lambda j: (0, 0, j))] * len(flat_grads),
        out_specs=[
            pl.BlockSpec((part, n_blocks, tile), lambda j: (0, 0, j)),
            pl.BlockSpec((rank, n_blocks, tile), lambda j: (0, 0, j)),
        ],
        out_shape=[
            jax.ShapeDtypeStruct((part, n_blocks, width), F32),
            jax.ShapeDtypeStruct((rank, n_blocks, width), F32),
        ],
        cost_estimate=pl.CostEstimate(
            flops=2 * n_groups * tokens * n_blocks * width * (part + rank),
            bytes_accessed=2 * n_groups * tokens * n_blocks * width
            + 4 * (part + rank) * n_blocks * width,
            transcendentals=0,
        ),
    )(*flat_rows, *lows, *flat_grads)


def doc_weights(segment_row, alive_count):
    slot_ids = jnp.arange(segment_row.shape[0], dtype=jnp.int32)
    is_alive = slot_ids < alive_count
    same_doc = (segment_row[:, None] == segment_row[None, :]) & is_alive[None, :]
    doc_length = jnp.sum(same_doc.astype(F32), axis=1)
    return (32.0 / (16.0 + doc_length)).astype(BF16)


def swap(value, axis, mask):
    return lax.ppermute(value, axis, [(s, s ^ mask) for s in range(lax.axis_size(axis))])


def row_total(partial_sum):
    mine = partial_sum.astype(BF16)
    if lax.axis_size("row") == 2:
        return mine.astype(F32) + swap(mine, "row", 1).astype(F32)
    return lax.psum(mine, "row").astype(F32)


def gather_groups(value, masks):
    held = [value]
    for mask in masks:
        arrived = []
        for x in held:
            arrived.append(swap(x, "dp", mask))
        held = held + arrived
    return held


def col_total(part, direct):
    if not direct:
        return lax.psum_scatter(part, "col", scatter_dimension=0, tiled=True).astype(F32)
    n_col = lax.axis_size("col")
    me = lax.axis_index("col")
    shards = part.reshape(n_col, part.shape[0] // n_col, part.shape[1])
    total = None
    for k in range(n_col):
        mine = lax.dynamic_index_in_dim(shards, me ^ k, 0, keepdims=False)
        if k:
            mine = swap(mine, "col", k)
        total = mine.astype(F32) if k == 0 else total + mine.astype(F32)
    return total


def local(
    source_rows, segments, send_slots, send_counts, block_weight, lowrank_in, lowrank_out, cotangent
):
    n_data = lax.axis_size("dp")
    n_col = lax.axis_size("col")
    my_data = lax.axis_index("dp")
    n_blocks, block_in, _ = block_weight.shape
    rank_width = lowrank_in.shape[2]
    group_rows = cotangent.shape[0]
    own_rows = group_rows // n_col
    count_table = send_counts[0]
    slot_table = send_slots[0]
    outgoing = jnp.take(source_rows, slot_table, axis=0)
    incoming = lax.all_to_all(outgoing, "dp", split_axis=0, concat_axis=0, tiled=True)
    capacity = slot_table.shape[1]
    arrivals = lax.dynamic_index_in_dim(count_table, my_data, 1, keepdims=False)
    starts = jnp.cumsum(arrivals) - arrivals
    positions = jnp.arange(own_rows, dtype=jnp.int32)
    sender = jnp.sum((starts[None, :] <= positions[:, None]).astype(jnp.int32), axis=1) - 1
    offset = positions - jnp.take(starts, sender)
    flat_index = sender * capacity + offset
    my_rows = jnp.take(incoming.reshape(n_data * capacity, incoming.shape[2]), flat_index, axis=0)

    segment_row, _ = lax.optimization_barrier((segments[0], my_rows))
    my_alive = jnp.sum(lax.dynamic_index_in_dim(count_table, my_data, 0, keepdims=False))
    weights = doc_weights(segment_row, my_alive)
    out_weights = jnp.take(weights, slot_table, axis=0)
    in_weights = lax.all_to_all(out_weights, "dp", split_axis=0, concat_axis=0, tiled=True)
    my_weights = jnp.take(in_weights.reshape(n_data * capacity), flat_index, axis=0)

    flat_in = lowrank_in.reshape(n_blocks * block_in, rank_width)
    own_part = jnp.dot(my_rows, flat_in, preferred_element_type=F32)
    own_low = row_total(own_part).astype(BF16)
    own_extra = jnp.concatenate(
        [own_low, jnp.broadcast_to(my_weights[:, None], (own_rows, 128))], axis=1
    )
    halves = 2
    half_width = n_blocks * block_in // halves
    panel_low = None
    panels = []
    for h in range(halves):
        piece = my_rows[:, h * half_width : (h + 1) * half_width]
        panels.append(lax.all_gather(piece, "col", axis=0, tiled=True))
        if h == 0:
            extra = lax.all_gather(own_extra, "col", axis=0, tiled=True)
            panel_low = extra[:, :rank_width]
            tok_weight = extra[:, rank_width : rank_width + 1].astype(F32)

    low_out_blocks = jnp.transpose(lowrank_out, (1, 0, 2))
    cot_blocks = jnp.transpose(cotangent, (1, 0, 2))

    masks = []
    bit = n_data // 2
    while bit:
        masks.append(bit)
        bit //= 2
    offsets = [0]
    for mask in masks:
        offsets = offsets + [k ^ mask for k in offsets]

    low_split = jnp.transpose(panel_low.reshape(group_rows, n_data, -1), (1, 0, 2))
    per_half = n_blocks // halves
    chunks = min(4, n_blocks)
    per_chunk = n_blocks // chunks
    acts, grads, in_terms, low_terms, row_parts = [], [], [], [], []
    me_array = jnp.full((1,), my_data, jnp.int32)
    direct = n_col <= 4
    group_slices = [[] for _ in offsets]
    for h in range(halves):
        row_parts.append(split_rows(me_array, panels[h], per_half, offsets))
        for at, k in enumerate(offsets):
            piece = row_parts[h][at]
            group_slices[at].append(swap(piece, "dp", k) if k else piece)
        for c in range(h * chunks // halves, (h + 1) * chunks // halves):
            act, grad, in_term, low_term = block_chunk(
                panels[h],
                c * per_chunk - h * per_half,
                block_weight,
                panel_low,
                low_out_blocks,
                cot_blocks,
                tok_weight,
                c * per_chunk,
                per_chunk,
            )
            acts.append(act)
            grads.append(gather_groups(grad, masks))
            in_terms.append(in_term)
            low_terms.append(low_term)

    group_lows = []
    for k in offsets:
        low_piece = lax.dynamic_index_in_dim(low_split, my_data ^ k, 0, keepdims=False)
        group_lows.append(swap(low_piece, "dp", k) if k else low_piece)

    own_low_term = col_total(sum(low_terms).astype(BF16), direct)
    low_grad = row_total(own_low_term).astype(BF16)
    half_chunks = chunks // halves
    terms = []
    for h in range(halves):
        part = jnp.concatenate(in_terms[h * half_chunks : (h + 1) * half_chunks], axis=1)
        terms.append(col_total(part, direct))
    own_term = jnp.concatenate(terms, axis=1).astype(F32)
    input_grad = (own_term + dot(low_grad, flat_in, 1, 1)).astype(BF16)

    act_out = jnp.transpose(jnp.concatenate(acts, axis=0), (1, 0, 2))
    by_group = [[grads[c][g] for c in range(chunks)] for g in range(n_data)]
    block_grad, out_grad = weight_grads(group_slices, group_lows, by_group)
    return (act_out, input_grad, block_grad, out_grad)


def solution(mesh):
    in_specs = (
        P(("dp", "col"), "row"),
        P(("dp", "col"), None),
        P(("dp", "col"), None, None),
        P("col", None, None),
        P("row", None, "col"),
        P("row", None, None),
        P(None, "row", "col"),
        P("dp", "row", "col"),
    )
    out_specs = (
        P("dp", "row", "col"),
        P(("dp", "col"), "row"),
        P("dp", "row", "col"),
        P("dp", "row", "col"),
    )

    return jax.shard_map(local, mesh=mesh, in_specs=in_specs, out_specs=out_specs, check_vma=False)
```

```python
import functools

import jax
import jax.numpy as jnp
from jax import lax
from jax.experimental import pallas as pl
from jax.experimental.pallas import tpu as pltpu
from jax.sharding import PartitionSpec as P


F32 = jnp.float32
BF16 = jnp.bfloat16


def dot(left, right, left_dim, right_dim):
    return lax.dot_general(
        left, right, (((left_dim,), (right_dim,)), ((), ())), preferred_element_type=F32
    )


def block_kernel(rows, weight, low, low_out, cot, tok_weight, act, grad, in_term, low_term):
    pre = dot(rows[...], weight[0], 1, 0) + dot(low[...], low_out[0], 1, 0)
    square = pre * pre
    tanh_val = jnp.tanh(0.7978845608 * (pre + 0.044715 * (square * pre)))
    half = 0.5 * (1.0 + tanh_val)
    act[0] = (pre * half).astype(BF16)
    slope = half + 0.5 * pre * (1.0 - tanh_val * tanh_val) * 0.7978845608 * (
        1.0 + 0.134145 * square
    )
    grad_pre = (tok_weight[...] * cot[0].astype(F32) * slope).astype(BF16)
    grad[0] = grad_pre
    in_term[...] = dot(grad_pre, weight[0], 1, 1).astype(BF16)
    part = dot(grad_pre, low_out[0], 1, 1)

    @pl.when(pl.program_id(0) == 0)
    def _():
        low_term[...] = part

    @pl.when(pl.program_id(0) > 0)
    def _():
        low_term[...] += part


def block_chunk(rows, row_base, weight, low, low_out, cot, tok_weight, base, count):
    tokens = rows.shape[0]
    _, width_in, width_out = weight.shape
    rank = low.shape[1]
    return pl.pallas_call(
        block_kernel,
        grid=(count,),
        in_specs=[
            pl.BlockSpec((tokens, width_in), lambda b: (0, row_base + b)),
            pl.BlockSpec((1, width_in, width_out), lambda b: (base + b, 0, 0)),
            pl.BlockSpec((tokens, rank), lambda b: (0, 0)),
            pl.BlockSpec((1, rank, width_out), lambda b: (base + b, 0, 0)),
            pl.BlockSpec((1, tokens, width_out), lambda b: (base + b, 0, 0)),
            pl.BlockSpec((tokens, 1), lambda b: (0, 0)),
        ],
        out_specs=[
            pl.BlockSpec((1, tokens, width_out), lambda b: (b, 0, 0)),
            pl.BlockSpec((1, tokens, width_out), lambda b: (b, 0, 0)),
            pl.BlockSpec((tokens, width_in), lambda b: (0, b)),
            pl.BlockSpec((tokens, rank), lambda b: (0, 0)),
        ],
        out_shape=[
            jax.ShapeDtypeStruct((count, tokens, width_out), BF16),
            jax.ShapeDtypeStruct((count, tokens, width_out), BF16),
            jax.ShapeDtypeStruct((tokens, count * width_in), BF16),
            jax.ShapeDtypeStruct((tokens, rank), F32),
        ],
        cost_estimate=pl.CostEstimate(
            flops=4 * count * tokens * width_out * (width_in + rank),
            bytes_accessed=2 * count * width_out * (width_in + rank + 3 * tokens),
            transcendentals=count * tokens * width_out,
        ),
    )(rows, weight, low, low_out, cot, tok_weight)


def split_kernel(n_parts, offsets, me, rows, *outs):
    part = outs[0].shape[2]
    for out, k in zip(outs, offsets):
        for e in range(n_parts):

            @pl.when((me[0] ^ k) == e)
            def _(out=out, e=e):
                out[0] = rows[:, e * part : (e + 1) * part]


def split_rows(me, rows, n_blocks, offsets):
    tokens, width = rows.shape
    n_parts = len(offsets)
    block_in = width // n_blocks
    part = block_in // n_parts
    return pl.pallas_call(
        functools.partial(split_kernel, n_parts, offsets),
        grid_spec=pltpu.PrefetchScalarGridSpec(
            num_scalar_prefetch=1,
            grid=(n_blocks,),
            in_specs=[pl.BlockSpec((tokens, block_in), lambda b, me: (0, b))],
            out_specs=[pl.BlockSpec((1, tokens, part), lambda b, me: (b, 0, 0))] * n_parts,
        ),
        out_shape=[jax.ShapeDtypeStruct((n_blocks, tokens, part), BF16)] * n_parts,
        cost_estimate=pl.CostEstimate(
            flops=0, bytes_accessed=4 * tokens * width, transcendentals=0
        ),
    )(me, rows)


def weight_kernel(n_groups, chunks, ready, *refs):
    rows = refs[:n_groups]
    lows = refs[n_groups : 2 * n_groups]
    refs = refs[2 * n_groups :]
    grads = refs[: n_groups * chunks]
    done = refs[n_groups * chunks : -2]
    block_out, low_out = refs[-2:]
    per_chunk = grads[0].shape[0]
    low_all = jnp.concatenate([x[...] for x in lows], axis=0)
    for b in range(ready):
        block_out[:, b, :] = done[0][b]
        low_out[:, b, :] = done[1][b]
    for b in range(per_chunk * chunks):
        grad = jnp.concatenate(
            [grads[g * chunks + b // per_chunk][b % per_chunk] for g in range(n_groups)], axis=0
        )
        row = jnp.concatenate([x[b] for x in rows], axis=0)
        block_sum = dot(row, grad, 0, 0)
        low_sum = dot(low_all, grad, 0, 0)
        if done:
            block_out[:, ready + b, :] = block_sum
            low_out[:, ready + b, :] = low_sum
        else:
            block_out[b] = block_sum
            low_out[b] = low_sum


def weight_grads(rows, lows, grads, done=()):
    n_groups = len(rows)
    chunks = len(grads[0])
    count, tokens, part = rows[0].shape
    per_chunk, _, width = grads[0][0].shape
    rank = lows[0].shape[1]
    tile = 256 if width % 256 == 0 else width
    flat_grads = [x for group in grads for x in group]
    ready = done[0].shape[0] if done else 0
    if done:
        shapes = [(part, ready + count, width), (rank, ready + count, width)]
        blocks = [(part, ready + count, tile), (rank, ready + count, tile)]
    else:
        shapes = [(count, part, width), (count, rank, width)]
        blocks = [(count, part, tile), (count, rank, tile)]
    return pl.pallas_call(
        functools.partial(weight_kernel, n_groups, chunks, ready),
        grid=(width // tile,),
        in_specs=[pl.BlockSpec((count, tokens, part), lambda j: (0, 0, 0))] * n_groups
        + [pl.BlockSpec((tokens, rank), lambda j: (0, 0))] * n_groups
        + [pl.BlockSpec((per_chunk, tokens, tile), lambda j: (0, 0, j))] * len(flat_grads)
        + [pl.BlockSpec((ready, x.shape[1], tile), lambda j: (0, 0, j)) for x in done],
        out_specs=[pl.BlockSpec(x, lambda j: (0, 0, j)) for x in blocks],
        out_shape=[jax.ShapeDtypeStruct(x, F32) for x in shapes],
        cost_estimate=pl.CostEstimate(
            flops=2 * n_groups * tokens * count * width * (part + rank),
            bytes_accessed=2 * n_groups * tokens * count * width
            + 4 * (part + rank) * (count + 2 * ready) * width,
            transcendentals=0,
        ),
    )(*rows, *lows, *flat_grads, *done)


def doc_weights(segment_row, alive_count):
    slot_ids = jnp.arange(segment_row.shape[0], dtype=jnp.int32)
    is_alive = slot_ids < alive_count
    same_doc = (segment_row[:, None] == segment_row[None, :]) & is_alive[None, :]
    doc_length = jnp.sum(same_doc.astype(F32), axis=1)
    return (32.0 / (16.0 + doc_length)).astype(BF16)


def swap(value, axis, mask):
    return lax.ppermute(value, axis, [(s, s ^ mask) for s in range(lax.axis_size(axis))])


def row_total(partial_sum):
    mine = partial_sum.astype(BF16)
    if lax.axis_size("row") == 2:
        return mine.astype(F32) + swap(mine, "row", 1).astype(F32)
    return lax.psum(mine, "row").astype(F32)


def gather_groups(value, masks):
    held = [value]
    for mask in masks:
        arrived = []
        for x in held:
            arrived.append(swap(x, "dp", mask))
        held = held + arrived
    return held


def col_gather(own, direct):
    if not direct:
        return lax.all_gather(own, "col", axis=0, tiled=True)
    n_col = lax.axis_size("col")
    me = lax.axis_index("col")
    size = own.shape[0]
    full = jnp.zeros((n_col * size, own.shape[1]), own.dtype)
    for k in range(n_col):
        piece = swap(own, "col", k) if k else own
        full = lax.dynamic_update_slice(full, piece, ((me ^ k) * size, 0))
    return full


def col_total(part, direct):
    if not direct:
        return lax.psum_scatter(part, "col", scatter_dimension=0, tiled=True).astype(F32)
    n_col = lax.axis_size("col")
    me = lax.axis_index("col")
    shards = part.reshape(n_col, part.shape[0] // n_col, part.shape[1])
    total = None
    for k in range(n_col):
        mine = lax.dynamic_index_in_dim(shards, me ^ k, 0, keepdims=False)
        if k:
            mine = swap(mine, "col", k)
        total = mine.astype(F32) if k == 0 else total + mine.astype(F32)
    return total


def local(
    source_rows, segments, send_slots, send_counts, block_weight, lowrank_in, lowrank_out, cotangent
):
    n_data = lax.axis_size("dp")
    n_col = lax.axis_size("col")
    my_data = lax.axis_index("dp")
    n_blocks, block_in, _ = block_weight.shape
    rank_width = lowrank_in.shape[2]
    group_rows = cotangent.shape[0]
    own_rows = group_rows // n_col
    count_table = send_counts[0]
    slot_table = send_slots[0]
    outgoing = jnp.take(source_rows, slot_table, axis=0)
    incoming = lax.all_to_all(outgoing, "dp", split_axis=0, concat_axis=0, tiled=True)
    capacity = slot_table.shape[1]
    arrivals = lax.dynamic_index_in_dim(count_table, my_data, 1, keepdims=False)
    starts = jnp.cumsum(arrivals) - arrivals
    positions = jnp.arange(own_rows, dtype=jnp.int32)
    sender = jnp.sum((starts[None, :] <= positions[:, None]).astype(jnp.int32), axis=1) - 1
    offset = positions - jnp.take(starts, sender)
    flat_index = sender * capacity + offset
    my_rows = jnp.take(incoming.reshape(n_data * capacity, incoming.shape[2]), flat_index, axis=0)

    flat_in = lowrank_in.reshape(n_blocks * block_in, rank_width)
    own_part = jnp.dot(my_rows, flat_in, preferred_element_type=F32).astype(BF16)
    segment_row, own_part, later_rows = lax.optimization_barrier((segments[0], own_part, my_rows))
    own_low = row_total(own_part).astype(BF16)
    my_alive = jnp.sum(lax.dynamic_index_in_dim(count_table, my_data, 0, keepdims=False))
    weights = doc_weights(segment_row, my_alive)
    out_weights = jnp.take(weights, slot_table, axis=0)
    in_weights = lax.all_to_all(out_weights, "dp", split_axis=0, concat_axis=0, tiled=True)
    my_weights = jnp.take(in_weights.reshape(n_data * capacity), flat_index, axis=0)
    own_extra = jnp.concatenate(
        [own_low, jnp.broadcast_to(my_weights[:, None], (own_rows, 128))], axis=1
    )
    direct = n_col <= 4
    if direct:
        lowrank_out, cotangent, own_extra = lax.optimization_barrier(
            (lowrank_out, cotangent, own_extra)
        )
    halves = 2
    half_width = n_blocks * block_in // halves
    panel_low = None
    panels = []
    for h in range(halves):
        piece = (later_rows if h else my_rows)[:, h * half_width : (h + 1) * half_width]
        panels.append(lax.all_gather(piece, "col", axis=0, tiled=True))
        if h == 0:
            extra = col_gather(own_extra, direct)
            panel_low = extra[:, :rank_width]
            tok_weight = extra[:, rank_width : rank_width + 1].astype(F32)

    low_out_blocks = jnp.transpose(lowrank_out, (1, 0, 2))
    cot_blocks = jnp.transpose(cotangent, (1, 0, 2))

    masks = []
    bit = n_data // 2
    while bit:
        masks.append(bit)
        bit //= 2
    offsets = [0]
    for mask in masks:
        offsets = offsets + [k ^ mask for k in offsets]

    low_split = jnp.transpose(panel_low.reshape(group_rows, n_data, -1), (1, 0, 2))
    per_half = n_blocks // halves
    chunks = min(4, n_blocks)
    per_chunk = n_blocks // chunks
    acts, grads, in_terms, low_terms, row_parts = [], [], [], [], []
    me_array = jnp.full((1,), my_data, jnp.int32)
    group_slices = [[] for _ in offsets]
    for h in range(halves):
        row_parts.append(split_rows(me_array, panels[h], per_half, offsets))
        for at, k in enumerate(offsets):
            piece = row_parts[h][at]
            group_slices[at].append(swap(piece, "dp", k) if k else piece)
        for c in range(h * chunks // halves, (h + 1) * chunks // halves):
            act, grad, in_term, low_term = block_chunk(
                panels[h],
                c * per_chunk - h * per_half,
                block_weight,
                panel_low,
                low_out_blocks,
                cot_blocks,
                tok_weight,
                c * per_chunk,
                per_chunk,
            )
            acts.append(act)
            grads.append(gather_groups(grad, masks))
            in_terms.append(in_term)
            low_terms.append(low_term)

    group_lows = []
    for k in offsets:
        low_piece = lax.dynamic_index_in_dim(low_split, my_data ^ k, 0, keepdims=False)
        group_lows.append(swap(low_piece, "dp", k) if k else low_piece)

    own_low_term = col_total(sum(low_terms).astype(BF16), direct)
    low_grad = row_total(own_low_term).astype(BF16)
    half_chunks = chunks // halves
    terms = []
    for h in range(halves):
        part = jnp.concatenate(in_terms[h * half_chunks : (h + 1) * half_chunks], axis=1)
        terms.append(col_total(part, direct))
    own_term = jnp.concatenate(terms, axis=1).astype(F32)
    input_grad = (own_term + dot(low_grad, flat_in, 1, 1)).astype(BF16)

    act_out = jnp.transpose(jnp.concatenate(acts, axis=0), (1, 0, 2))
    done = ()
    for h in range(halves):
        by_group = [
            [grads[c][g] for c in range(h * half_chunks, (h + 1) * half_chunks)]
            for g in range(n_data)
        ]
        done = weight_grads([x[h] for x in group_slices], group_lows, by_group, done)
    block_grad, out_grad = done
    return (act_out, input_grad, block_grad, out_grad)


def solution(mesh):
    in_specs = (
        P(("dp", "col"), "row"),
        P(("dp", "col"), None),
        P(("dp", "col"), None, None),
        P("col", None, None),
        P("row", None, "col"),
        P("row", None, None),
        P(None, "row", "col"),
        P("dp", "row", "col"),
    )
    out_specs = (
        P("dp", "row", "col"),
        P(("dp", "col"), "row"),
        P("dp", "row", "col"),
        P("dp", "row", "col"),
    )

    return jax.shard_map(local, mesh=mesh, in_specs=in_specs, out_specs=out_specs, check_vma=False)
```
